256 devices in a mesh: sub: 4 (over z_hi), row: 16 (over y, x), col: 4 (over z_lo, core).
Axes of the slice: x: 4, y: 4, z: 8 (z_hi: 4, z_lo: 2; z = z_hi * 2 + z_lo), core: 2. Of those that a mesh axis runs over, the one named last changes fastest.
Arguments:
- front_in: float32 [12288, 12288], P('row', ('sub', 'col')), as said below
- child_updates: float32 [4, 8192, 8192], P('sub', 'row', 'col'), as said below
- pattern: int32 [4, 32, 32], P('sub', 'row', 'col'), may hold values from 0 to 1, as said below
- child_map: int32 [4, 32], replicated, may hold values from 0 to 47, as said below
- pivot_inverse: float32 [1024, 1024], replicated, as said below
Outputs:
- front_out: float32 [12288, 12288], P('row', ('sub', 'col'))
The draws below stay inside these ranges and needn't reach their ends.
Inputs may be any that keep to these rules, and one draw needn't show every extreme that they name: front_in is symmetric. Each child_updates[s] is symmetric. Each pattern[s] is symmetric. child_map[s] is strictly increasing, and child_map[s, i] // 3 equals i // 2. pivot_inverse is lower triangular with a positive diagonal.
All inputs are finite; a program needn't handle non-finite values.
Results may differ from the reference program's by a relative error of at most 0.000053.
Values sent between devices are 32-bit elements; how exact they have to be, the bound alone decides.
No kernel may reach another device: no remote copies, remote signals or barrier semaphores. Data moves between devices by JAX's collectives and lax.ppermute only.
A program may use at most 128 MiB of HBM per device.

```python
import jax
import jax.numpy as jnp
from jax import lax

BLK = 256
FRONT = 12288
CHILD = 8192
PANEL = 1024
GROUPS = 16
CHILDREN = 4
FBLOCKS = 48
CBLOCKS = 32


def symmetric_field(key, shape):
    first = jax.random.fold_in(key, 0)
    base = jnp.clip(jax.random.normal(first, shape, dtype=jnp.float32), -6.0, 6.0)
    return ((base + jnp.swapaxes(base, -1, -2)) * 0.70710678).astype(jnp.float32)


def draw_front_in(key, part):
    field = symmetric_field(jax.random.fold_in(key, 11), (FRONT, FRONT))
    return field.astype(jnp.float32)


def draw_child_updates(key, part):
    return symmetric_field(jax.random.fold_in(key, 21), (CHILDREN, CHILD, CHILD))


def draw_pattern(key, part):
    levels = jax.random.randint(jax.random.fold_in(key, 31), (CHILDREN, CBLOCKS, CBLOCKS), 0, 4)
    upper = (levels < 3).astype(jnp.int32)
    rows_idx = jnp.arange(CBLOCKS)[:, None]
    cols_idx = jnp.arange(CBLOCKS)[None, :]
    return jnp.where((rows_idx <= cols_idx)[None], upper, jnp.swapaxes(upper, 1, 2)).astype(jnp.int32)


def draw_child_map(key, part):
    fgroup = FBLOCKS // GROUPS
    cgroup = CBLOCKS // GROUPS
    omitted = jax.random.randint(key, (CHILDREN, GROUPS), 0, fgroup)
    omitted = omitted.at[0, 0].set(fgroup - 1).at[0, GROUPS - 1].set(0)
    slots = jnp.arange(cgroup, dtype=jnp.int32)
    chosen = slots[None, None, :] + (slots[None, None, :] >= omitted[:, :, None]).astype(jnp.int32)
    starts = (jnp.arange(GROUPS, dtype=jnp.int32) * fgroup)[None, :, None]
    return (starts + chosen).reshape(CHILDREN, CBLOCKS).astype(jnp.int32)


def draw_pivot_inverse(key, part):
    first, second = jax.random.split(key, 2)
    offdiag = 0.006 * jax.random.normal(first, (PANEL, PANEL), dtype=jnp.float32)
    diagonal = jnp.exp(jax.random.uniform(second, (PANEL,), minval=jnp.log(0.1), maxval=jnp.log(0.2)))
    rows_idx = jnp.arange(PANEL)[:, None]
    cols_idx = jnp.arange(PANEL)[None, :]
    strict = jnp.where(rows_idx > cols_idx, offdiag, 0.0)
    return (strict + jnp.where(rows_idx == cols_idx, diagonal[:, None], 0.0)).astype(jnp.float32)


def setup_inputs(seed: int = 0) -> dict:
    seeds = jax.random.split(jax.random.key(seed), 6)
    front_in = draw_front_in(jax.random.fold_in(seeds[5], 71), 0)
    child_updates = draw_child_updates(jax.random.fold_in(seeds[5], 71), 0)
    pattern = draw_pattern(jax.random.fold_in(seeds[5], 71), 0)
    child_map = draw_child_map(jax.random.fold_in(seeds[5], 71), 0)
    pivot_inverse = draw_pivot_inverse(jax.random.fold_in(seeds[5], 71), 0)
    return {"front_in": front_in, "child_updates": child_updates, "pattern": pattern, "child_map": child_map, "pivot_inverse": pivot_inverse}


def reference(front_in, child_updates, pattern, child_map, pivot_inverse):
    fblocks = FRONT // BLK
    cblocks = CHILD // BLK
    blocks = front_in.reshape(fblocks, BLK, fblocks, BLK).transpose(0, 2, 1, 3)
    for source in range(CHILDREN):
        update = child_updates[source].reshape(cblocks, BLK, cblocks, BLK).transpose(0, 2, 1, 3)
        update = update * pattern[source][:, :, None, None].astype(jnp.float32)
        targets = child_map[source]
        blocks = blocks.at[targets[:, None], targets[None, :]].add(update)
    assembled = blocks.transpose(0, 2, 1, 3).reshape(FRONT, FRONT)
    factor = jnp.dot(assembled[PANEL:, :PANEL], pivot_inverse.T, precision=lax.Precision.HIGHEST, preferred_element_type=jnp.float32)
    trailing = assembled[PANEL:, PANEL:] - jnp.dot(factor, factor.T, precision=lax.Precision.HIGHEST, preferred_element_type=jnp.float32)
    return assembled.at[PANEL:, :PANEL].set(factor).at[PANEL:, PANEL:].set(trailing)
```

```python
import jax
import jax.numpy as jnp
from jax import lax
from jax.experimental import pallas as pl
from jax.experimental.pallas import tpu as pltpu
from jax.sharding import PartitionSpec as P

BLK = 256
PANEL = 1024
RING = ("sub", "col")
MESH = ("sub", "row", "col")
SMEM = pl.BlockSpec(memory_space=pltpu.SMEM)
VMEM = pl.BlockSpec(memory_space=pltpu.VMEM)
PARAMS = pltpu.CompilerParams(vmem_limit_bytes=56 * 1024 * 1024)
F32 = jnp.float32


def split(x):
    hi = x.astype(jnp.bfloat16)
    return hi, (x - hi.astype(F32)).astype(jnp.bfloat16)


def times_transposed(left, right):
    lh, ll = split(left)
    rh, rl = split(right)

    def dot(a, b):
        return lax.dot_general(a, b, (((1,), (1,)), ((), ())), preferred_element_type=F32)

    return dot(lh, rl) + dot(ll, rh) + dot(lh, rh)


def place(cmap, child, group, slot):
    target = 3 * group + slot
    first = (cmap[child, 2 * group] == target).astype(jnp.int32)
    second = (cmap[child, 2 * group + 1] == target).astype(jnp.int32)
    return second, first + second


def mask_kernel(ids, pat, *refs):
    i = pl.program_id(0)
    for j in range(4):
        group = (ids[0] + j) % 4
        for b in range(2):
            cols = pl.ds(b * BLK, BLK)
            refs[4 + j][:, cols] = refs[j][0, :, cols] * pat[i, 2 * group + b].astype(F32)


def masked_groups(ids, pat, child):
    def group(j):
        return pl.BlockSpec((1, BLK, 2 * BLK), lambda i, ids, pat: (0, i, (ids[0] + j) % 4))

    return pl.pallas_call(
        mask_kernel,
        grid_spec=pltpu.PrefetchScalarGridSpec(
            num_scalar_prefetch=2,
            grid=(2,),
            in_specs=[group(j) for j in range(4)],
            out_specs=[pl.BlockSpec((BLK, 2 * BLK), lambda i, ids, pat: (i, 0))] * 4,
        ),
        out_shape=[jax.ShapeDtypeStruct((2 * BLK, 2 * BLK), F32)] * 4,
        compiler_params=PARAMS,
        name="masked_groups",
    )(ids, pat, child, child, child, child)


def panel_kernel(ids, pat, cmap, child, front, last, *outs):
    s = ids[0]
    row = ids[1]
    root = (s == 0).astype(F32)
    cols = [place(cmap, s, 0, q) for q in range(3)]
    cols.append((jnp.int32(2), (cmap[s, 2] == 3).astype(jnp.int32)))
    for p in range(3):
        a, a_ok = place(cmap, s, row, p)
        for q in range(4):
            b, b_ok = cols[q]
            weight = (pat[a, b] * a_ok * b_ok).astype(F32)
            for d in range(8):
                z = (2 * s + d) % 8
                src = pl.multiple_of(a * BLK + z * 32, 32)
                own = pl.ds(pl.multiple_of(p * BLK + z * 32, 32), 32)
                value = child[0, pl.ds(src, 32), pl.ds(pl.multiple_of(b * BLK, BLK), BLK)] * weight
                kept = front[own, pl.ds(q * BLK, BLK)] if q < 3 else last[own, :]
                outs[d][p, :, pl.ds(q * BLK, BLK)] = value + kept * root


def panel_slices(ids, pat, cmap, child, front, last):
    return pl.pallas_call(
        panel_kernel,
        grid=(1,),
        in_specs=[
            SMEM,
            SMEM,
            SMEM,
            pl.BlockSpec((1, 2 * BLK, 3 * BLK), lambda i: (0, 0, 0)),
            pl.BlockSpec((3 * BLK, 3 * BLK), lambda i: (0, 0)),
            pl.BlockSpec((3 * BLK, BLK), lambda i: (0, 0)),
        ],
        out_specs=[pl.BlockSpec((3, 32, PANEL), lambda i: (0, 0, 0))] * 8,
        out_shape=[jax.ShapeDtypeStruct((3, 32, PANEL), F32)] * 8,
        compiler_params=PARAMS,
        name="panel_slices",
    )(ids, pat, cmap, child, front, last)


def factor_kernel(ids, *refs):
    parts, pivot, out = refs[:8], refs[8], refs[9]
    odd = (2 * ids[0] + ids[2] // 2) % 2

    def total(which):
        value = parts[which][...]
        for m in range(1, 4):
            value = value + parts[which + 2 * m][...]
        return value.reshape(96, PANEL)

    rows = jnp.where(odd == 1, total(1), total(0))
    out[...] = times_transposed(rows, pivot[...]).reshape(3, 32, PANEL)


def factor_slice(ids, parts, pivot):
    return pl.pallas_call(
        factor_kernel,
        in_specs=[SMEM] + [VMEM] * 9,
        out_specs=VMEM,
        out_shape=jax.ShapeDtypeStruct((3, 32, PANEL), F32),
        compiler_params=PARAMS,
        name="factor_slice",
    )(ids, *parts, pivot)


def final_kernel(ids, cmap, front, r0, r1, r2, r3, left, right, out):
    p = pl.program_id(0)
    q = pl.program_id(1)
    row = ids[1]
    group = 4 * ids[0] + ids[2]
    value = front[...]
    for j, ref in enumerate((r0, r1, r2, r3)):
        child = (ids[2] - j + 4) % 4
        ok = place(cmap, child, row, p)[1] * place(cmap, child, group, q)[1]
        value = value + ref[...] * ok.astype(F32)
    row_block = 3 * row + p
    col_block = 3 * group + q
    out[...] = value

    @pl.when((row_block >= 4) & (col_block < 4))
    def _():
        cols = pl.ds(pl.multiple_of(jnp.minimum(col_block, 3) * BLK, BLK), BLK)
        out[...] = left[:, 0, :, cols].reshape(BLK, BLK)

    @pl.when((row_block >= 4) & (col_block >= 4))
    def _():
        out[...] = value - times_transposed(left[...].reshape(BLK, PANEL), right[...].reshape(BLK, PANEL))


def final(ids, cmap, front, arrived, left, right):
    def from_child(j):
        def where(p, q, ids, cmap):
            child = (ids[2] - j + 4) % 4
            return (
                place(cmap, child, ids[1], p)[0],
                place(cmap, child, 4 * ids[0] + ids[2], q)[0],
            )

        return pl.BlockSpec((BLK, BLK), where)

    tile = pl.BlockSpec((BLK, BLK), lambda p, q, ids, cmap: (p, q))
    return pl.pallas_call(
        final_kernel,
        grid_spec=pltpu.PrefetchScalarGridSpec(
            num_scalar_prefetch=2,
            grid=(3, 3),
            in_specs=[tile]
            + [from_child(j) for j in range(4)]
            + [
                pl.BlockSpec((8, 1, 32, PANEL), lambda p, q, ids, cmap: (0, p, 0, 0)),
                pl.BlockSpec((16, 1, 16, PANEL), lambda p, q, ids, cmap: (0, q, 0, 0)),
            ],
            out_specs=tile,
        ),
        out_shape=jax.ShapeDtypeStruct((3 * BLK, 3 * BLK), F32),
        compiler_params=PARAMS,
        name="final",
    )(ids, cmap, front, *arrived, left, right)


def shards(front_in, child_updates, pattern, child_map, pivot_inverse):
    sub = lax.axis_index("sub")
    row = lax.axis_index("row")
    col = lax.axis_index("col")
    ids = jnp.stack([sub, row, col]).astype(jnp.int32)
    core = col % 2
    z = 2 * sub + col // 2
    pat = pattern[0]

    last = lax.ppermute(front_in[:, :BLK], RING, [(1, 0)])
    slices = panel_slices(ids, pat, child_map, child_updates, front_in, last)
    parts = [slices[0]]
    for d in range(1, 8):
        parts.append(lax.ppermute(slices[d], RING, [(4 * s, 2 * ((2 * s + d) % 8)) for s in range(4)]))

    sent = masked_groups(ids, pat, child_updates)
    arrived = [
        lax.ppermute(
            sent[j], RING, [(4 * s + c, 4 * c + (s + j) % 4) for s in range(4) for c in range(4)]
        )
        for j in range(4)
    ]

    mine = factor_slice(ids, parts, pivot_inverse)
    other = lax.ppermute(mine, RING, [(2 * k, 2 * k + 1) for k in range(8)])
    mine = jnp.where(core == 0, mine, other)

    half = lax.dynamic_slice_in_dim(mine, core * 16, 16, 1)
    turn = [
        ((s * 16 + r) * 4 + c, ((r // 4) * 16 + 4 * s + c) * 4 + r % 4)
        for s in range(4)
        for r in range(16)
        for c in range(4)
    ]
    right = lax.all_gather(lax.ppermute(half, MESH, turn), "row", axis=0)

    onward = [(2 * k, 2 * ((k + 1) % 8)) for k in range(8)]
    onward += [(2 * k + 1, 2 * ((k - 1) % 8) + 1) for k in range(8)]
    swap = [(k, k ^ 1) for k in range(16)]
    step = 1 - 2 * core
    left = jnp.zeros((8,) + mine.shape, F32)
    left = lax.dynamic_update_slice_in_dim(left, mine[None], z, 0)
    piece = mine
    for t in range(1, 5):
        piece = lax.ppermute(piece, RING, onward)
        left = lax.dynamic_update_slice_in_dim(left, piece[None], (z - t * step) % 8, 0)
        if t < 4:
            swapped = lax.ppermute(piece, RING, swap)
            left = lax.dynamic_update_slice_in_dim(left, swapped[None], (z + t * step) % 8, 0)
    return final(ids, child_map, front_in, arrived, left, right)


def solution(mesh):
    in_specs = (P("row", ("sub", "col")), P("sub", "row", "col"), P("sub", "row", "col"), P(), P())
    out_specs = P("row", ("sub", "col"))
    return jax.shard_map(shards, mesh=mesh, in_specs=in_specs, out_specs=out_specs, check_vma=False)
```

```python
import jax
import jax.numpy as jnp
from jax import lax
from jax.experimental import pallas as pl
from jax.experimental.pallas import tpu as pltpu
from jax.sharding import PartitionSpec as P

BLK = 256
PANEL = 1024
RING = ("sub", "col")
MESH = ("sub", "row", "col")
SMEM = pl.BlockSpec(memory_space=pltpu.SMEM)
VMEM = pl.BlockSpec(memory_space=pltpu.VMEM)
PARAMS = pltpu.CompilerParams(vmem_limit_bytes=56 * 1024 * 1024)
F32 = jnp.float32


def split(x):
    hi = x.astype(jnp.bfloat16)
    return hi, (x - hi.astype(F32)).astype(jnp.bfloat16)


def times_transposed(left, right):
    lh, ll = split(left)
    rh, rl = split(right)

    def dot(a, b):
        return lax.dot_general(a, b, (((1,), (1,)), ((), ())), preferred_element_type=F32)

    return dot(lh, rl) + dot(ll, rh) + dot(lh, rh)


def place(cmap, child, group, slot):
    target = 3 * group + slot
    first = (cmap[child, 2 * group] == target).astype(jnp.int32)
    second = (cmap[child, 2 * group + 1] == target).astype(jnp.int32)
    return second, first + second


def mask_kernel(ids, pat, *refs):
    i = pl.program_id(0)
    for j in range(4):
        group = (ids[0] + j) % 4
        for b in range(2):
            cols = pl.ds(b * BLK, BLK)
            refs[4 + j][:, cols] = refs[j][0, :, cols] * pat[i, 2 * group + b].astype(F32)


def masked_groups(ids, pat, child):
    def group(j):
        return pl.BlockSpec((1, BLK, 2 * BLK), lambda i, ids, pat: (0, i, (ids[0] + j) % 4))

    return pl.pallas_call(
        mask_kernel,
        grid_spec=pltpu.PrefetchScalarGridSpec(
            num_scalar_prefetch=2,
            grid=(2,),
            in_specs=[group(j) for j in range(4)],
            out_specs=[pl.BlockSpec((BLK, 2 * BLK), lambda i, ids, pat: (i, 0))] * 4,
        ),
        out_shape=[jax.ShapeDtypeStruct((2 * BLK, 2 * BLK), F32)] * 4,
        compiler_params=PARAMS,
        name="masked_groups",
    )(ids, pat, child, child, child, child)


def panel_kernel(ids, pat, cmap, child, front, last, *outs):
    s = ids[0]
    row = ids[1]
    root = (s == 0).astype(F32)
    cols = [place(cmap, s, 0, q) for q in range(3)]
    cols.append((jnp.int32(2), (cmap[s, 2] == 3).astype(jnp.int32)))
    for p in range(3):
        a, a_ok = place(cmap, s, row, p)
        for q in range(4):
            b, b_ok = cols[q]
            weight = (pat[a, b] * a_ok * b_ok).astype(F32)
            for d in range(8):
                z = (2 * s + d) % 8
                src = pl.multiple_of(a * BLK + z * 32, 32)
                own = pl.ds(pl.multiple_of(p * BLK + z * 32, 32), 32)
                value = child[0, pl.ds(src, 32), pl.ds(pl.multiple_of(b * BLK, BLK), BLK)] * weight
                kept = front[own, pl.ds(q * BLK, BLK)] if q < 3 else last[own, :]
                outs[d][p, :, pl.ds(q * BLK, BLK)] = value + kept * root


def panel_slices(ids, pat, cmap, child, front, last):
    return pl.pallas_call(
        panel_kernel,
        grid=(1,),
        in_specs=[
            SMEM,
            SMEM,
            SMEM,
            pl.BlockSpec((1, 2 * BLK, 3 * BLK), lambda i: (0, 0, 0)),
            pl.BlockSpec((3 * BLK, 3 * BLK), lambda i: (0, 0)),
            pl.BlockSpec((3 * BLK, BLK), lambda i: (0, 0)),
        ],
        out_specs=[pl.BlockSpec((3, 32, PANEL), lambda i: (0, 0, 0))] * 8,
        out_shape=[jax.ShapeDtypeStruct((3, 32, PANEL), F32)] * 8,
        compiler_params=PARAMS,
        name="panel_slices",
    )(ids, pat, cmap, child, front, last)


def factor_kernel(ids, *refs):
    parts, pivot, out = refs[:8], refs[8], refs[9]
    odd = (2 * ids[0] + ids[2] // 2) % 2

    def total(which):
        value = parts[which][...]
        for m in range(1, 4):
            value = value + parts[which + 2 * m][...]
        return value.reshape(96, PANEL)

    rows = jnp.where(odd == 1, total(1), total(0))
    out[...] = times_transposed(rows, pivot[...]).reshape(3, 32, PANEL)


def factor_slice(ids, parts, pivot):
    return pl.pallas_call(
        factor_kernel,
        in_specs=[SMEM] + [VMEM] * 9,
        out_specs=VMEM,
        out_shape=jax.ShapeDtypeStruct((3, 32, PANEL), F32),
        compiler_params=PARAMS,
        name="factor_slice",
    )(ids, *parts, pivot)


def region(ids, p, q):
    row_block = 3 * ids[1] + p
    col_block = 3 * (4 * ids[0] + ids[2]) + q
    return row_block >= 4, col_block


def sender(ids, j):
    return (ids[2] - j + 4) % 4


def lands(ids, cmap, j, p, q):
    child = sender(ids, j)
    group = 4 * ids[0] + ids[2]
    return (place(cmap, child, ids[1], p)[1] * place(cmap, child, group, q)[1]).astype(F32)


def arrival(j):
    def where(p, q, ids, cmap):
        child = sender(ids, j)
        return (
            place(cmap, child, ids[1], p)[0],
            place(cmap, child, 4 * ids[0] + ids[2], q)[0],
        )

    return pl.BlockSpec((BLK, BLK), where)


TILE = pl.BlockSpec((BLK, BLK), lambda p, q, ids, cmap: (p, q))


def update_kernel(ids, cmap, front, r0, r1, r2, *refs):
    left, right, out = refs[:3]
    left_hi, left_lo, right_hi, right_lo = refs[3:]
    p = pl.program_id(0)
    q = pl.program_id(1)

    @pl.when(q == 0)
    def _():
        hi, lo = split(left[...].reshape(BLK, PANEL))
        left_hi[...] = hi
        left_lo[...] = lo

    @pl.when(p == 0)
    def _():
        hi, lo = split(right[...].reshape(BLK, PANEL))
        right_hi[q] = hi
        right_lo[q] = lo

    value = front[...]
    for j, ref in enumerate((r0, r1, r2)):
        value = value + ref[...] * lands(ids, cmap, j, p, q)
    below, col_block = region(ids, p, q)
    out[...] = value

    @pl.when(below & (col_block < 4))
    def _():
        cols = pl.ds(pl.multiple_of(jnp.minimum(col_block, 3) * BLK, BLK), BLK)
        out[...] = left[:, 0, :, cols].reshape(BLK, BLK)

    @pl.when(below & (col_block >= 4))
    def _():
        def dot(a, b):
            return lax.dot_general(a, b, (((1,), (1,)), ((), ())), preferred_element_type=F32)

        lh, ll, rh, rl = left_hi[...], left_lo[...], right_hi[q], right_lo[q]
        out[...] = value - (dot(lh, rl) + dot(ll, rh) + dot(lh, rh))


def update(ids, cmap, front, arrived, left, right):
    return pl.pallas_call(
        update_kernel,
        grid_spec=pltpu.PrefetchScalarGridSpec(
            num_scalar_prefetch=2,
            grid=(3, 3),
            in_specs=[TILE]
            + [arrival(j) for j in range(3)]
            + [pl.BlockSpec((16, 1, 16, PANEL), lambda p, q, ids, cmap: (0, p, 0, 0))]
            + [
                pl.BlockSpec(
                    (16, 1, 16, PANEL), lambda p, q, ids, cmap: (0, jnp.where(p == 0, q, 2), 0, 0)
                )
            ],
            out_specs=TILE,
            scratch_shapes=[
                pltpu.VMEM((BLK, PANEL), jnp.bfloat16),
                pltpu.VMEM((BLK, PANEL), jnp.bfloat16),
                pltpu.VMEM((3, BLK, PANEL), jnp.bfloat16),
                pltpu.VMEM((3, BLK, PANEL), jnp.bfloat16),
            ],
        ),
        out_shape=jax.ShapeDtypeStruct((3 * BLK, 3 * BLK), F32),
        compiler_params=PARAMS,
        name="update",
    )(ids, cmap, front, *arrived, left, right)


def finish_kernel(ids, cmap, partial, r3, out):
    p = pl.program_id(0)
    q = pl.program_id(1)
    below, col_block = region(ids, p, q)
    adds = jnp.where(below & (col_block < 4), 0.0, lands(ids, cmap, 3, p, q))
    out[...] = partial[...] + r3[...] * adds


def finish(ids, cmap, partial, last):
    return pl.pallas_call(
        finish_kernel,
        grid_spec=pltpu.PrefetchScalarGridSpec(
            num_scalar_prefetch=2,
            grid=(3, 3),
            in_specs=[TILE, arrival(3)],
            out_specs=TILE,
        ),
        out_shape=jax.ShapeDtypeStruct((3 * BLK, 3 * BLK), F32),
        compiler_params=PARAMS,
        name="finish",
    )(ids, cmap, partial, last)


def shards(front_in, child_updates, pattern, child_map, pivot_inverse):
    sub = lax.axis_index("sub")
    row = lax.axis_index("row")
    col = lax.axis_index("col")
    ids = jnp.stack([sub, row, col]).astype(jnp.int32)
    core = col % 2
    pat = pattern[0]

    def send(j):
        return lax.ppermute(
            sent[j], RING, [(4 * s + c, 4 * c + (s + j) % 4) for s in range(4) for c in range(4)]
        )

    last = lax.ppermute(front_in[:, :BLK], RING, [(1, 0)])
    sent = masked_groups(ids, pat, child_updates)
    slices = panel_slices(ids, pat, child_map, child_updates, front_in, last)
    parts = [slices[0]]
    for d in range(1, 8):
        parts.append(lax.ppermute(slices[d], RING, [(4 * s, 2 * ((2 * s + d) % 8)) for s in range(4)]))
    parts, sent = lax.optimization_barrier((parts, sent))
    arrived = [send(j) for j in range(4)]

    mine = factor_slice(ids, parts, pivot_inverse)
    other = lax.ppermute(mine, RING, [(2 * k, 2 * k + 1) for k in range(8)])
    mine = jnp.where(core == 0, mine, other)

    half = lax.dynamic_slice_in_dim(mine, core * 16, 16, 1)
    turn = [
        ((s * 16 + r) * 4 + c, ((r // 4) * 16 + 4 * s + c) * 4 + r % 4)
        for s in range(4)
        for r in range(16)
        for c in range(4)
    ]
    turned = lax.ppermute(half, MESH, turn)
    right = lax.all_to_all(jnp.broadcast_to(turned, (16,) + turned.shape), "row", 0, 0)
    left = lax.all_gather(half, RING, axis=0)
    partial = update(ids, child_map, front_in, arrived[:3], left, right)
    return finish(ids, child_map, partial, arrived[3])


def solution(mesh):
    in_specs = (P("row", ("sub", "col")), P("sub", "row", "col"), P("sub", "row", "col"), P(), P())
    out_specs = P("row", ("sub", "col"))
    return jax.shard_map(shards, mesh=mesh, in_specs=in_specs, out_specs=out_specs, check_vma=False)
```

```python
import jax
import jax.numpy as jnp
from jax import lax
from jax.experimental import pallas as pl
from jax.experimental.pallas import tpu as pltpu
from jax.sharding import PartitionSpec as P

BLK = 256
PANEL = 1024
RING = ("sub", "col")
MESH = ("sub", "row", "col")
SMEM = pl.BlockSpec(memory_space=pltpu.SMEM)
VMEM = pl.BlockSpec(memory_space=pltpu.VMEM)
PARAMS = pltpu.CompilerParams(vmem_limit_bytes=56 * 1024 * 1024)
F32 = jnp.float32


def split(x):
    hi = x.astype(jnp.bfloat16)
    return hi, (x - hi.astype(F32)).astype(jnp.bfloat16)


def place(cmap, child, group, slot):
    target = 3 * group + slot
    first = (cmap[child, 2 * group] == target).astype(jnp.int32)
    second = (cmap[child, 2 * group + 1] == target).astype(jnp.int32)
    return second, first + second


def mask_kernel(ids, pat, *refs):
    i = pl.program_id(0)
    for j in range(4):
        group = (ids[0] + j) % 4
        for b in range(2):
            cols = pl.ds(b * BLK, BLK)
            refs[4 + j][:, cols] = refs[j][0, :, cols] * pat[i, 2 * group + b].astype(F32)


def masked_groups(ids, pat, child):
    def group(j):
        return pl.BlockSpec((1, BLK, 2 * BLK), lambda i, ids, pat: (0, i, (ids[0] + j) % 4))

    return pl.pallas_call(
        mask_kernel,
        grid_spec=pltpu.PrefetchScalarGridSpec(
            num_scalar_prefetch=2,
            grid=(2,),
            in_specs=[group(j) for j in range(4)],
            out_specs=[pl.BlockSpec((BLK, 2 * BLK), lambda i, ids, pat: (i, 0))] * 4,
        ),
        out_shape=[jax.ShapeDtypeStruct((2 * BLK, 2 * BLK), F32)] * 4,
        compiler_params=PARAMS,
        name="masked_groups",
    )(ids, pat, child, child, child, child)


def panel_kernel(ids, pat, cmap, child, front, last, *outs):
    s = ids[0]
    row = ids[1]
    root = (s == 0).astype(F32)
    cols = [place(cmap, s, 0, q) for q in range(3)]
    cols.append((jnp.int32(2), (cmap[s, 2] == 3).astype(jnp.int32)))
    for p in range(3):
        a, a_ok = place(cmap, s, row, p)
        for q in range(4):
            b, b_ok = cols[q]
            weight = (pat[a, b] * a_ok * b_ok).astype(F32)
            for d in range(4):
                t = (s + d) % 4
                src = pl.multiple_of(a * BLK + t * 64, 64)
                own = pl.ds(pl.multiple_of(p * BLK + t * 64, 64), 64)
                value = child[0, pl.ds(src, 64), pl.ds(pl.multiple_of(b * BLK, BLK), BLK)] * weight
                kept = front[own, pl.ds(q * BLK, BLK)] if q < 3 else last[own, :]
                outs[d][p, :, pl.ds(q * BLK, BLK)] = value + kept * root


def panel_slices(ids, pat, cmap, child, front, last):
    return pl.pallas_call(
        panel_kernel,
        grid=(1,),
        in_specs=[
            SMEM,
            SMEM,
            SMEM,
            pl.BlockSpec((1, 2 * BLK, 3 * BLK), lambda i: (0, 0, 0)),
            pl.BlockSpec((3 * BLK, 3 * BLK), lambda i: (0, 0)),
            pl.BlockSpec((3 * BLK, BLK), lambda i: (0, 0)),
        ],
        out_specs=[pl.BlockSpec((3, 64, PANEL), lambda i: (0, 0, 0))] * 4,
        out_shape=[jax.ShapeDtypeStruct((3, 64, PANEL), F32)] * 4,
        compiler_params=PARAMS,
        name="panel_slices",
    )(ids, pat, cmap, child, front, last)


def pivot_kernel(pivot, hi, lo):
    hi[...], lo[...] = split(pivot[...])


def split_pivot(pivot):
    return pl.pallas_call(
        pivot_kernel,
        in_specs=[VMEM],
        out_specs=[VMEM, VMEM],
        out_shape=[jax.ShapeDtypeStruct((PANEL, PANEL), jnp.bfloat16)] * 2,
        compiler_params=PARAMS,
        name="split_pivot",
    )(pivot)


def dot(a, b):
    return lax.dot_general(a, b, (((1,), (1,)), ((), ())), preferred_element_type=F32)


def factor_kernel(*refs):
    parts, pivot_hi, pivot_lo, outs = refs[:4], refs[4], refs[5], refs[6:]
    value = parts[0][...]
    for ref in parts[1:]:
        value = value + ref[...]
    hi, lo = split(value.reshape(192, PANEL))
    ph, po = pivot_hi[...], pivot_lo[...]
    factor = (dot(hi, po) + dot(lo, ph) + dot(hi, ph)).reshape(3, 64, PANEL)
    for k in range(4):
        outs[k][...] = factor[:, 16 * k : 16 * k + 16]


def factor_slices(parts, pivot):
    return pl.pallas_call(
        factor_kernel,
        in_specs=[VMEM] * 6,
        out_specs=[VMEM] * 4,
        out_shape=[jax.ShapeDtypeStruct((3, 16, PANEL), F32)] * 4,
        compiler_params=PARAMS,
        name="factor_slices",
    )(*parts, *pivot)


def region(ids, p, q):
    row_block = 3 * ids[1] + p
    col_block = 3 * (4 * ids[0] + ids[2]) + q
    return row_block >= 4, col_block


def sender(ids, j):
    return (ids[2] - j + 4) % 4


def lands(ids, cmap, j, p, q):
    child = sender(ids, j)
    group = 4 * ids[0] + ids[2]
    return (place(cmap, child, ids[1], p)[1] * place(cmap, child, group, q)[1]).astype(F32)


def update_kernel(ids, assembled, *refs):
    left, right, out = refs[:3]
    left_hi, left_lo, right_hi, right_lo = refs[3:]
    p = pl.program_id(0)
    q = pl.program_id(1)

    @pl.when(q == 0)
    def _():
        hi, lo = split(left[...].reshape(BLK, PANEL))
        left_hi[...] = hi
        left_lo[...] = lo

    @pl.when(p == 0)
    def _():
        hi, lo = split(right[...].reshape(BLK, PANEL))
        right_hi[q] = hi
        right_lo[q] = lo

    value = assembled[...]
    below, col_block = region(ids, p, q)
    out[...] = value

    @pl.when(below & (col_block < 4))
    def _():
        cols = pl.ds(pl.multiple_of(jnp.minimum(col_block, 3) * BLK, BLK), BLK)
        out[...] = left[:, 0, :, cols].reshape(BLK, BLK)

    @pl.when(below & (col_block >= 4))
    def _():
        lh, ll, rh, rl = left_hi[...], left_lo[...], right_hi[q], right_lo[q]
        out[...] = value - (dot(lh, rl) + dot(ll, rh) + dot(lh, rh))


def update(ids, assembled, left, right):
    tile = pl.BlockSpec((BLK, BLK), lambda p, q, ids: (p, q))
    return pl.pallas_call(
        update_kernel,
        grid_spec=pltpu.PrefetchScalarGridSpec(
            num_scalar_prefetch=1,
            grid=(3, 3),
            in_specs=[tile]
            + [pl.BlockSpec((16, 1, 16, PANEL), lambda p, q, ids: (0, p, 0, 0))]
            + [
                pl.BlockSpec(
                    (16, 1, 16, PANEL), lambda p, q, ids: (0, jnp.where(p == 0, q, 2), 0, 0)
                )
            ],
            out_specs=tile,
            scratch_shapes=[
                pltpu.VMEM((BLK, PANEL), jnp.bfloat16),
                pltpu.VMEM((BLK, PANEL), jnp.bfloat16),
                pltpu.VMEM((3, BLK, PANEL), jnp.bfloat16),
                pltpu.VMEM((3, BLK, PANEL), jnp.bfloat16),
            ],
        ),
        out_shape=jax.ShapeDtypeStruct((3 * BLK, 3 * BLK), F32),
        compiler_params=PARAMS,
        name="update",
    )(ids, assembled, left, right)


def finish_kernel(ids, cmap, partial, r0, r1, r2, r3, r4, out):
    p = pl.program_id(0)
    group = 4 * ids[0] + ids[2]
    for q in range(3):
        cols = pl.ds(q * BLK, BLK)
        below, col_block = region(ids, p, q)
        kept = jnp.where(below & (col_block < 4), 0.0, 1.0)
        value = partial[:, cols]
        for j, ref in ((0, r0), (1, r1), (2, r2), (3, r3), (2, r4)):
            b = place(cmap, sender(ids, j), group, q)[0]
            src = pl.ds(pl.multiple_of(b * BLK, BLK), BLK)
            value = value + ref[:, src] * (lands(ids, cmap, j, p, q) * kept)
        out[:, cols] = value


def finish(ids, cmap, partial, arrived):
    def arrival(j):
        return pl.BlockSpec(
            (BLK, 2 * BLK), lambda p, ids, cmap: (place(cmap, sender(ids, j), ids[1], p)[0], 0)
        )

    band = pl.BlockSpec((BLK, 3 * BLK), lambda p, ids, cmap: (p, 0))
    return pl.pallas_call(
        finish_kernel,
        grid_spec=pltpu.PrefetchScalarGridSpec(
            num_scalar_prefetch=2,
            grid=(3,),
            in_specs=[band] + [arrival(j) for j in (0, 1, 2, 3, 2)],
            out_specs=band,
        ),
        out_shape=jax.ShapeDtypeStruct((3 * BLK, 3 * BLK), F32),
        compiler_params=PARAMS,
        name="finish",
    )(ids, cmap, partial, *arrived)


def shards(front_in, child_updates, pattern, child_map, pivot_inverse):
    sub = lax.axis_index("sub")
    row = lax.axis_index("row")
    col = lax.axis_index("col")
    ids = jnp.stack([sub, row, col]).astype(jnp.int32)
    pat = pattern[0]

    def at(s, r, c):
        return (s * 16 + r) * 4 + c

    def send(j):
        pairs = []
        for s in range(4):
            for r in range(16):
                for c in range(4):
                    group = 4 * c + (s + j) % 4
                    if (r < 2 or group > 0) and (s, group) not in ((3, 5), (0, 10)):
                        pairs.append((at(s, r, c), at(c, r, (s + j) % 4)))
        return lax.ppermute(sent[j], MESH, pairs)

    last = lax.ppermute(front_in[:, :BLK], RING, [(1, 0)])
    sent = masked_groups(ids, pat, child_updates)
    slices = panel_slices(ids, pat, child_map, child_updates, front_in, last)
    parts = [slices[0]]
    for d in range(1, 4):
        parts.append(lax.ppermute(slices[d], RING, [(4 * s, 4 * ((s + d) % 4)) for s in range(4)]))
    pieces = factor_slices(parts, split_pivot(pivot_inverse))
    mine = pieces[0]
    others = [lax.ppermute(pieces[k], RING, [(4 * s, 4 * s + k) for s in range(4)]) for k in range(1, 4)]
    mine = jnp.where(col == 0, mine, others[0] + others[1] + others[2])

    leg = lax.ppermute(
        sent[2],
        MESH,
        [(at(3, r, 1), at(2, r, 2)) for r in range(16)] + [(at(0, r, 2), at(1, r, 1)) for r in range(16)],
    )
    mine, leg = lax.optimization_barrier((mine, leg))

    turn = [
        (at(s, r, c), at(r // 4, 4 * s + c, r % 4)) for s in range(4) for r in range(16) for c in range(4)
    ]
    turned = lax.ppermute(mine, MESH, turn)
    turned, sent, leg = lax.optimization_barrier((turned, sent, leg))
    relayed = lax.ppermute(
        leg, MESH, [(at(s, r, s), at(3 - s, r, 3 - s)) for s in (1, 2) for r in range(16)]
    )

    def spread(turned):
        return lax.all_to_all(jnp.broadcast_to(turned, (16,) + turned.shape), "row", 0, 0)

    right = lax.cond(
        child_map[0, 0] >= 0, spread, lambda turned: jnp.zeros((16,) + turned.shape, F32), turned
    )
    left = lax.all_gather(mine, RING, axis=0)
    partial = update(ids, front_in, left, right)
    return finish(ids, child_map, partial, [send(j) for j in range(4)] + [relayed])


def solution(mesh):
    in_specs = (P("row", ("sub", "col")), P("sub", "row", "col"), P("sub", "row", "col"), P(), P())
    out_specs = P("row", ("sub", "col"))
    return jax.shard_map(shards, mesh=mesh, in_specs=in_specs, out_specs=out_specs, check_vma=False)
```

```python
import jax
import jax.numpy as jnp
from jax import lax
from jax.experimental import pallas as pl
from jax.experimental.pallas import tpu as pltpu
from jax.sharding import PartitionSpec as P

BLK = 256
PANEL = 1024
RING = ("sub", "col")
MESH = ("sub", "row", "col")
SMEM = pl.BlockSpec(memory_space=pltpu.SMEM)
VMEM = pl.BlockSpec(memory_space=pltpu.VMEM)
PARAMS = pltpu.CompilerParams(vmem_limit_bytes=56 * 1024 * 1024)
F32 = jnp.float32


def split(x):
    hi = x.astype(jnp.bfloat16)
    return hi, (x - hi.astype(F32)).astype(jnp.bfloat16)


def place(cmap, child, group, slot):
    target = 3 * group + slot
    first = (cmap[child, 2 * group] == target).astype(jnp.int32)
    second = (cmap[child, 2 * group + 1] == target).astype(jnp.int32)
    return second, first + second


def mask_kernel(ids, pat, *refs):
    i = pl.program_id(0)
    for j in range(4):
        group = (ids[0] + j) % 4
        for b in range(2):
            cols = pl.ds(b * BLK, BLK)
            refs[4 + j][:, cols] = refs[j][0, :, cols] * pat[i, 2 * group + b].astype(F32)


def masked_groups(ids, pat, child):
    def group(j):
        return pl.BlockSpec((1, BLK, 2 * BLK), lambda i, ids, pat: (0, i, (ids[0] + j) % 4))

    return pl.pallas_call(
        mask_kernel,
        grid_spec=pltpu.PrefetchScalarGridSpec(
            num_scalar_prefetch=2,
            grid=(2,),
            in_specs=[group(j) for j in range(4)],
            out_specs=[pl.BlockSpec((BLK, 2 * BLK), lambda i, ids, pat: (i, 0))] * 4,
        ),
        out_shape=[jax.ShapeDtypeStruct((2 * BLK, 2 * BLK), F32)] * 4,
        compiler_params=PARAMS,
        name="masked_groups",
    )(ids, pat, child, child, child, child)


def panel_kernel(ids, pat, cmap, child, front, last, *outs):
    s = ids[0]
    row = ids[1]
    root = (s == 0).astype(F32)
    cols = [place(cmap, s, 0, q) for q in range(3)]
    cols.append((jnp.int32(2), (cmap[s, 2] == 3).astype(jnp.int32)))
    for p in range(3):
        a, a_ok = place(cmap, s, row, p)
        for q in range(4):
            b, b_ok = cols[q]
            weight = (pat[a, b] * a_ok * b_ok).astype(F32)
            for d in range(4):
                t = (s + d) % 4
                src = pl.multiple_of(a * BLK + t * 64, 64)
                own = pl.ds(pl.multiple_of(p * BLK + t * 64, 64), 64)
                value = child[0, pl.ds(src, 64), pl.ds(pl.multiple_of(b * BLK, BLK), BLK)] * weight
                kept = front[own, pl.ds(q * BLK, BLK)] if q < 3 else last[own, :]
                outs[d][p, :, pl.ds(q * BLK, BLK)] = value + kept * root


def panel_slices(ids, pat, cmap, child, front, last):
    return pl.pallas_call(
        panel_kernel,
        grid=(1,),
        in_specs=[
            SMEM,
            SMEM,
            SMEM,
            pl.BlockSpec((1, 2 * BLK, 3 * BLK), lambda i: (0, 0, 0)),
            pl.BlockSpec((3 * BLK, 3 * BLK), lambda i: (0, 0)),
            pl.BlockSpec((3 * BLK, BLK), lambda i: (0, 0)),
        ],
        out_specs=[pl.BlockSpec((3, 64, PANEL), lambda i: (0, 0, 0))] * 4,
        out_shape=[jax.ShapeDtypeStruct((3, 64, PANEL), F32)] * 4,
        compiler_params=PARAMS,
        name="panel_slices",
    )(ids, pat, cmap, child, front, last)


def pivot_kernel(pivot, hi, lo):
    hi[...], lo[...] = split(pivot[...].T)


def split_pivot(pivot):
    return pl.pallas_call(
        pivot_kernel,
        in_specs=[VMEM],
        out_specs=[VMEM, VMEM],
        out_shape=[jax.ShapeDtypeStruct((PANEL, PANEL), jnp.bfloat16)] * 2,
        compiler_params=PARAMS,
        name="split_pivot",
    )(pivot)


def dot(a, b):
    return lax.dot_general(a, b, (((1,), (1,)), ((), ())), preferred_element_type=F32)


def times(a, b):
    return lax.dot_general(a, b, (((1,), (0,)), ((), ())), preferred_element_type=F32)


def factor_kernel(*refs):
    parts, pivot_hi, pivot_lo, outs = refs[:4], refs[4], refs[5], refs[6:]
    value = parts[0][...]
    for ref in parts[1:]:
        value = value + ref[...]
    hi, lo = split(value.reshape(192, PANEL))
    ph, po = pivot_hi[...], pivot_lo[...]
    factor = (times(hi, po) + times(lo, ph) + times(hi, ph)).reshape(3, 64, PANEL)
    for k in range(4):
        outs[k][...] = factor[:, 16 * k : 16 * k + 16]


def factor_slices(parts, pivot):
    return pl.pallas_call(
        factor_kernel,
        in_specs=[VMEM] * 6,
        out_specs=[VMEM] * 4,
        out_shape=[jax.ShapeDtypeStruct((3, 16, PANEL), F32)] * 4,
        compiler_params=PARAMS,
        name="factor_slices",
    )(*parts, *pivot)


def region(ids, p, q):
    row_block = 3 * ids[1] + p
    col_block = 3 * (4 * ids[0] + ids[2]) + q
    return row_block >= 4, col_block


def sender(ids, j):
    if j == 5:
        return jnp.where(ids[0] == 1, 2, jnp.where(ids[0] == 2, 1, ids[0]))
    return (ids[2] - j + 4) % 4


def lands(ids, cmap, j, p, q):
    child = sender(ids, j)
    group = 4 * ids[0] + ids[2]
    return (place(cmap, child, ids[1], p)[1] * place(cmap, child, group, q)[1]).astype(F32)


def update_kernel(ids, cmap, front, early, *refs):
    left, right, out = refs[:3]
    left_hi, left_lo, right_hi, right_lo = refs[3:]
    p = pl.program_id(0)
    q = pl.program_id(1)

    @pl.when(q == 0)
    def _():
        hi, lo = split(left[...].reshape(BLK, PANEL))
        left_hi[...] = hi
        left_lo[...] = lo

    @pl.when(p == 0)
    def _():
        hi, lo = split(right[...].reshape(BLK, PANEL))
        right_hi[q] = hi
        right_lo[q] = lo

    value = front[...] + early[...] * lands(ids, cmap, 5, p, q)
    below, col_block = region(ids, p, q)
    out[...] = value

    @pl.when(below & (col_block < 4))
    def _():
        cols = pl.ds(pl.multiple_of(jnp.minimum(col_block, 3) * BLK, BLK), BLK)
        out[...] = left[:, 0, :, cols].reshape(BLK, BLK)

    @pl.when(below & (col_block >= 4))
    def _():
        lh, ll, rh, rl = left_hi[...], left_lo[...], right_hi[q], right_lo[q]
        out[...] = value - (dot(lh, rl) + dot(ll, rh) + dot(lh, rh))


def update(ids, cmap, front, early, left, right):
    def where(p, q, ids, cmap):
        child = sender(ids, 5)
        return (
            place(cmap, child, ids[1], p)[0],
            place(cmap, child, 4 * ids[0] + ids[2], q)[0],
        )

    tile = pl.BlockSpec((BLK, BLK), lambda p, q, ids, cmap: (p, q))
    return pl.pallas_call(
        update_kernel,
        grid_spec=pltpu.PrefetchScalarGridSpec(
            num_scalar_prefetch=2,
            grid=(3, 3),
            in_specs=[tile, pl.BlockSpec((BLK, BLK), where)]
            + [pl.BlockSpec((16, 1, 16, PANEL), lambda p, q, ids, cmap: (0, p, 0, 0))]
            + [
                pl.BlockSpec(
                    (16, 1, 16, PANEL), lambda p, q, ids, cmap: (0, jnp.where(p == 0, q, 2), 0, 0)
                )
            ],
            out_specs=tile,
            scratch_shapes=[
                pltpu.VMEM((BLK, PANEL), jnp.bfloat16),
                pltpu.VMEM((BLK, PANEL), jnp.bfloat16),
                pltpu.VMEM((3, BLK, PANEL), jnp.bfloat16),
                pltpu.VMEM((3, BLK, PANEL), jnp.bfloat16),
            ],
        ),
        out_shape=jax.ShapeDtypeStruct((3 * BLK, 3 * BLK), F32),
        compiler_params=PARAMS,
        name="update",
    )(ids, cmap, front, early, left, right)


def finish_kernel(ids, cmap, partial, r0, r1, r2, r3, r4, out):
    p = pl.program_id(0)
    group = 4 * ids[0] + ids[2]
    for q in range(3):
        cols = pl.ds(q * BLK, BLK)
        below, col_block = region(ids, p, q)
        kept = jnp.where(below & (col_block < 4), 0.0, 1.0)
        value = partial[:, cols]
        for j, ref in ((0, r0), (1, r1), (2, r2), (3, r3), (2, r4)):
            b = place(cmap, sender(ids, j), group, q)[0]
            src = pl.ds(pl.multiple_of(b * BLK, BLK), BLK)
            value = value + ref[:, src] * (lands(ids, cmap, j, p, q) * kept)
        out[:, cols] = value


def finish(ids, cmap, partial, arrived):
    def arrival(j):
        return pl.BlockSpec(
            (BLK, 2 * BLK), lambda p, ids, cmap: (place(cmap, sender(ids, j), ids[1], p)[0], 0)
        )

    band = pl.BlockSpec((BLK, 3 * BLK), lambda p, ids, cmap: (p, 0))
    return pl.pallas_call(
        finish_kernel,
        grid_spec=pltpu.PrefetchScalarGridSpec(
            num_scalar_prefetch=2,
            grid=(3,),
            in_specs=[band] + [arrival(j) for j in (0, 1, 2, 3, 2)],
            out_specs=band,
        ),
        out_shape=jax.ShapeDtypeStruct((3 * BLK, 3 * BLK), F32),
        compiler_params=PARAMS,
        name="finish",
    )(ids, cmap, partial, *arrived)


def shards(front_in, child_updates, pattern, child_map, pivot_inverse):
    sub = lax.axis_index("sub")
    row = lax.axis_index("row")
    col = lax.axis_index("col")
    ids = jnp.stack([sub, row, col]).astype(jnp.int32)
    pat = pattern[0]

    def at(s, r, c):
        return (s * 16 + r) * 4 + c

    ahead = [
        [(0, 0, 2, (0, 2)), (3, 3, 1, (3, 1)), (1, 2, 1, (2, 1)), (2, 1, 2, (1, 2)), (3, 1, 1, (2, 2)), (0, 2, 2, (1, 1))],
        [(0, 0, 3, (0, 3)), (3, 3, 0, (3, 0)), (1, 2, 0, (2, 0)), (2, 1, 3, (1, 3))],
    ]
    gone = {(s, c, k) for part in ahead for s, c, k, _ in part}

    def send(j):
        pairs = []
        for s in range(4):
            for r in range(16):
                for c in range(4):
                    k = (s + j) % 4
                    if (r < 2 or c + k > 0) and (s, c, k) not in gone:
                        pairs.append((at(s, r, c), at(c, r, k)))
        return lax.ppermute(sent[j], MESH, pairs)

    def send_ahead(block, part):
        return lax.ppermute(
            block, MESH, [(at(s, r, c), at(t[0], r, t[1])) for s, c, _, t in part for r in range(16)]
        )

    last = lax.ppermute(front_in[:, :BLK], RING, [(1, 0)])
    sent = masked_groups(ids, pat, child_updates)
    slices = panel_slices(ids, pat, child_map, child_updates, front_in, last)
    parts = [slices[0]]
    for d in range(1, 4):
        parts.append(lax.ppermute(slices[d], RING, [(4 * s, 4 * ((s + d) % 4)) for s in range(4)]))
    pieces = factor_slices(parts, split_pivot(pivot_inverse))
    mine = pieces[0]
    others = [lax.ppermute(pieces[k], RING, [(4 * s, 4 * s + k) for s in range(4)]) for k in range(1, 4)]
    mine = jnp.where(col == 0, mine, others[0] + others[1] + others[2])

    leg = send_ahead(jnp.where((sub == 0) | (sub == 3), sent[2], sent[0]), ahead[0])
    rest = send_ahead(jnp.where(sub < 2, sent[3], sent[1]), ahead[1])
    mine, leg, rest = lax.optimization_barrier((mine, leg, rest))
    early = jnp.where(col == jnp.where(sub < 2, 2, 1), leg, rest)

    turn = [
        (at(s, r, c), at(r // 4, 4 * s + c, r % 4)) for s in range(4) for r in range(16) for c in range(4)
    ]
    turned = lax.ppermute(mine, MESH, turn)
    turned, sent, leg = lax.optimization_barrier((turned, sent, leg))
    relayed = lax.ppermute(
        leg, MESH, [(at(s, r, s), at(3 - s, r, 3 - s)) for s in (1, 2) for r in range(16)]
    )

    def spread(turned):
        return lax.all_to_all(jnp.broadcast_to(turned, (16,) + turned.shape), "row", 0, 0)

    right = lax.cond(
        child_map[0, 0] >= 0, spread, lambda turned: jnp.zeros((16,) + turned.shape, F32), turned
    )
    left = lax.all_gather(mine, RING, axis=0)
    partial = update(ids, child_map, front_in, early, left, right)
    return finish(ids, child_map, partial, [send(j) for j in range(4)] + [relayed])


def solution(mesh):
    in_specs = (P("row", ("sub", "col")), P("sub", "row", "col"), P("sub", "row", "col"), P(), P())
    out_specs = P("row", ("sub", "col"))
    return jax.shard_map(shards, mesh=mesh, in_specs=in_specs, out_specs=out_specs, check_vma=False)
```

```python
import jax
import jax.numpy as jnp
from jax import lax
from jax.experimental import pallas as pl
from jax.experimental.pallas import tpu as pltpu
from jax.sharding import PartitionSpec as P

BLK = 256
PANEL = 1024
RING = ("sub", "col")
MESH = ("sub", "row", "col")
SMEM = pl.BlockSpec(memory_space=pltpu.SMEM)
VMEM = pl.BlockSpec(memory_space=pltpu.VMEM)
PARAMS = pltpu.CompilerParams(vmem_limit_bytes=56 * 1024 * 1024)
F32 = jnp.float32


def split(x):
    hi = x.astype(jnp.bfloat16)
    return hi, (x - hi.astype(F32)).astype(jnp.bfloat16)


def place(cmap, child, group, slot):
    target = 3 * group + slot
    first = (cmap[child, 2 * group] == target).astype(jnp.int32)
    second = (cmap[child, 2 * group + 1] == target).astype(jnp.int32)
    return second, first + second


def mask_kernel(ids, pat, *refs):
    i = pl.program_id(0)
    for j in range(4):
        group = (ids[0] + j) % 4
        for b in range(2):
            cols = pl.ds(b * BLK, BLK)
            refs[4 + j][:, cols] = refs[j][0, :, cols] * pat[i, 2 * group + b].astype(F32)


def masked_groups(ids, pat, child):
    def group(j):
        return pl.BlockSpec((1, BLK, 2 * BLK), lambda i, ids, pat: (0, i, (ids[0] + j) % 4))

    return pl.pallas_call(
        mask_kernel,
        grid_spec=pltpu.PrefetchScalarGridSpec(
            num_scalar_prefetch=2,
            grid=(2,),
            in_specs=[group(j) for j in range(4)],
            out_specs=[pl.BlockSpec((BLK, 2 * BLK), lambda i, ids, pat: (i, 0))] * 4,
        ),
        out_shape=[jax.ShapeDtypeStruct((2 * BLK, 2 * BLK), F32)] * 4,
        compiler_params=PARAMS,
        name="masked_groups",
    )(ids, pat, child, child, child, child)


def panel_kernel(ids, pat, cmap, child, front, last, *outs):
    s = ids[0]
    row = ids[1]
    root = (s == 0).astype(F32)
    cols = [place(cmap, s, 0, q) for q in range(3)]
    cols.append((jnp.int32(2), (cmap[s, 2] == 3).astype(jnp.int32)))
    for p in range(3):
        a, a_ok = place(cmap, s, row, p)
        for q in range(4):
            b, b_ok = cols[q]
            weight = (pat[a, b] * a_ok * b_ok).astype(F32)
            for d in range(4):
                t = (s + d) % 4
                src = pl.multiple_of(a * BLK + t * 64, 64)
                own = pl.ds(pl.multiple_of(p * BLK + t * 64, 64), 64)
                value = child[0, pl.ds(src, 64), pl.ds(pl.multiple_of(b * BLK, BLK), BLK)] * weight
                kept = front[own, pl.ds(q * BLK, BLK)] if q < 3 else last[own, :]
                outs[d][p, :, pl.ds(q * BLK, BLK)] = value + kept * root


def panel_slices(ids, pat, cmap, child, front, last):
    return pl.pallas_call(
        panel_kernel,
        grid=(1,),
        in_specs=[
            SMEM,
            SMEM,
            SMEM,
            pl.BlockSpec((1, 2 * BLK, 3 * BLK), lambda i: (0, 0, 0)),
            pl.BlockSpec((3 * BLK, 3 * BLK), lambda i: (0, 0)),
            pl.BlockSpec((3 * BLK, BLK), lambda i: (0, 0)),
        ],
        out_specs=[pl.BlockSpec((3, 64, PANEL), lambda i: (0, 0, 0))] * 4,
        out_shape=[jax.ShapeDtypeStruct((3, 64, PANEL), F32)] * 4,
        compiler_params=PARAMS,
        name="panel_slices",
    )(ids, pat, cmap, child, front, last)


def pivot_kernel(pivot, hi, lo):
    hi[...], lo[...] = split(pivot[...].T)


def split_pivot(pivot):
    return pl.pallas_call(
        pivot_kernel,
        in_specs=[VMEM],
        out_specs=[VMEM, VMEM],
        out_shape=[jax.ShapeDtypeStruct((PANEL, PANEL), jnp.bfloat16)] * 2,
        compiler_params=PARAMS,
        name="split_pivot",
    )(pivot)


def dot(a, b):
    return lax.dot_general(a, b, (((1,), (1,)), ((), ())), preferred_element_type=F32)


def times(a, b):
    return lax.dot_general(a, b, (((1,), (0,)), ((), ())), preferred_element_type=F32)


def factor_kernel(*refs):
    parts, pivot_hi, pivot_lo, outs = refs[:4], refs[4], refs[5], refs[6:]
    value = parts[0][...]
    for ref in parts[1:]:
        value = value + ref[...]
    hi, lo = split(value.reshape(192, PANEL))
    ph, po = pivot_hi[...], pivot_lo[...]
    factor = (times(hi, po) + times(lo, ph) + times(hi, ph)).reshape(3, 64, PANEL)
    for k in range(4):
        outs[k][...] = factor[:, 16 * k : 16 * k + 16]


def factor_slices(parts, pivot):
    return pl.pallas_call(
        factor_kernel,
        in_specs=[VMEM] * 6,
        out_specs=[VMEM] * 4,
        out_shape=[jax.ShapeDtypeStruct((3, 16, PANEL), F32)] * 4,
        compiler_params=PARAMS,
        name="factor_slices",
    )(*parts, *pivot)


def region(ids, p, q):
    row_block = 3 * ids[1] + p
    col_block = 3 * (4 * ids[0] + ids[2]) + q
    return row_block >= 4, col_block


def sender(ids, j):
    if j == 5:
        return jnp.where(ids[0] == 1, 2, jnp.where(ids[0] == 2, 1, ids[0]))
    return (ids[2] - j + 4) % 4


def lands(ids, cmap, j, p, q):
    child = sender(ids, j)
    group = 4 * ids[0] + ids[2]
    return (place(cmap, child, ids[1], p)[1] * place(cmap, child, group, q)[1]).astype(F32)


def update_kernel(ids, cmap, front, early, *refs):
    left, right, out = refs[:3]
    left_hi, left_lo, right_hi, right_lo = refs[3:]
    p = pl.program_id(0)
    q = pl.program_id(1)

    @pl.when(q == 0)
    def _():
        hi, lo = split(left[...].reshape(BLK, PANEL))
        left_hi[...] = hi
        left_lo[...] = lo

    @pl.when(p == 0)
    def _():
        hi, lo = split(right[...].reshape(BLK, PANEL))
        right_hi[q] = hi
        right_lo[q] = lo

    value = front[...] + early[...] * lands(ids, cmap, 5, p, q)
    below, col_block = region(ids, p, q)
    out[...] = value

    @pl.when(below & (col_block < 4))
    def _():
        cols = pl.ds(pl.multiple_of(jnp.minimum(col_block, 3) * BLK, BLK), BLK)
        out[...] = left[:, 0, :, cols].reshape(BLK, BLK)

    @pl.when(below & (col_block >= 4))
    def _():
        lh, ll, rh, rl = left_hi[...], left_lo[...], right_hi[q], right_lo[q]
        out[...] = value - (dot(lh, rl) + dot(ll, rh) + dot(lh, rh))


def update(ids, cmap, front, early, left, right):
    def where(p, q, ids, cmap):
        child = sender(ids, 5)
        return (
            place(cmap, child, ids[1], p)[0],
            place(cmap, child, 4 * ids[0] + ids[2], q)[0],
        )

    tile = pl.BlockSpec((BLK, BLK), lambda p, q, ids, cmap: (p, q))
    return pl.pallas_call(
        update_kernel,
        grid_spec=pltpu.PrefetchScalarGridSpec(
            num_scalar_prefetch=2,
            grid=(3, 3),
            in_specs=[tile, pl.BlockSpec((BLK, BLK), where)]
            + [pl.BlockSpec((16, 1, 16, PANEL), lambda p, q, ids, cmap: (0, p, 0, 0))]
            + [
                pl.BlockSpec(
                    (16, 1, 16, PANEL), lambda p, q, ids, cmap: (0, jnp.where(p == 0, q, 2), 0, 0)
                )
            ],
            out_specs=tile,
            scratch_shapes=[
                pltpu.VMEM((BLK, PANEL), jnp.bfloat16),
                pltpu.VMEM((BLK, PANEL), jnp.bfloat16),
                pltpu.VMEM((3, BLK, PANEL), jnp.bfloat16),
                pltpu.VMEM((3, BLK, PANEL), jnp.bfloat16),
            ],
        ),
        out_shape=jax.ShapeDtypeStruct((3 * BLK, 3 * BLK), F32),
        compiler_params=PARAMS,
        name="update",
    )(ids, cmap, front, early, left, right)


def finish_kernel(ids, cmap, partial, r0, r1, r2, r3, r4, out):
    p = pl.program_id(0)
    group = 4 * ids[0] + ids[2]
    for q in range(3):
        cols = pl.ds(q * BLK, BLK)
        below, col_block = region(ids, p, q)
        kept = jnp.where(below & (col_block < 4), 0.0, 1.0)
        value = partial[:, cols]
        for j, ref in ((0, r0), (1, r1), (2, r2), (3, r3), (2, r4)):
            b = place(cmap, sender(ids, j), group, q)[0]
            src = pl.ds(pl.multiple_of(b * BLK, BLK), BLK)
            value = value + ref[:, src] * (lands(ids, cmap, j, p, q) * kept)
        out[:, cols] = value


def finish(ids, cmap, partial, arrived):
    def arrival(j):
        return pl.BlockSpec(
            (BLK, 2 * BLK), lambda p, ids, cmap: (place(cmap, sender(ids, j), ids[1], p)[0], 0)
        )

    band = pl.BlockSpec((BLK, 3 * BLK), lambda p, ids, cmap: (p, 0))
    return pl.pallas_call(
        finish_kernel,
        grid_spec=pltpu.PrefetchScalarGridSpec(
            num_scalar_prefetch=2,
            grid=(3,),
            in_specs=[band] + [arrival(j) for j in (0, 1, 2, 3, 2)],
            out_specs=band,
        ),
        out_shape=jax.ShapeDtypeStruct((3 * BLK, 3 * BLK), F32),
        compiler_params=PARAMS,
        name="finish",
    )(ids, cmap, partial, *arrived)


def shards(front_in, child_updates, pattern, child_map, pivot_inverse):
    sub = lax.axis_index("sub")
    row = lax.axis_index("row")
    col = lax.axis_index("col")
    ids = jnp.stack([sub, row, col]).astype(jnp.int32)
    pat = pattern[0]

    def at(s, r, c):
        return (s * 16 + r) * 4 + c

    ahead = [
        [(0, 0, 2, (0, 2)), (3, 3, 1, (3, 1)), (1, 2, 1, (2, 1)), (2, 1, 2, (1, 2)), (3, 1, 1, (2, 2)), (0, 2, 2, (1, 1))],
        [(0, 0, 3, (0, 3)), (3, 3, 0, (3, 0)), (1, 2, 0, (2, 0)), (2, 1, 3, (1, 3))],
    ]
    gone = {(s, c, k) for part in ahead for s, c, k, _ in part}

    def send(j):
        pairs = []
        for s in range(4):
            for r in range(16):
                for c in range(4):
                    k = (s + j) % 4
                    if (r < 2 or c + k > 0) and (s, c, k) not in gone:
                        pairs.append((at(s, r, c), at(c, r, k)))
        return lax.ppermute(sent[j], MESH, pairs)

    def send_ahead(block, part):
        return lax.ppermute(
            block, MESH, [(at(s, r, c), at(t[0], r, t[1])) for s, c, _, t in part for r in range(16)]
        )

    last = lax.ppermute(front_in[:, :BLK], RING, [(1, 0)])
    sent = masked_groups(ids, pat, child_updates)
    slices = panel_slices(ids, pat, child_map, child_updates, front_in, last)
    parts = [slices[0]]
    for d in range(1, 4):
        parts.append(lax.ppermute(slices[d], RING, [(4 * s, 4 * ((s + d) % 4)) for s in range(4)]))
    pieces = factor_slices(parts, split_pivot(pivot_inverse))
    mine = pieces[0]
    others = [lax.ppermute(pieces[k], RING, [(4 * s, 4 * s + k) for s in range(4)]) for k in range(1, 4)]
    mine = jnp.where(col == 0, mine, others[0] + others[1] + others[2])

    leg = send_ahead(jnp.where((sub == 0) | (sub == 3), sent[2], sent[0]), ahead[0])
    rest = send_ahead(jnp.where(sub < 2, sent[3], sent[1]), ahead[1])
    mine, leg, rest, sent = lax.optimization_barrier((mine, leg, rest, sent))
    relayed = lax.ppermute(
        leg, MESH, [(at(s, r, s), at(3 - s, r, 3 - s)) for s in (1, 2) for r in range(16)]
    )
    arrived = {j: send(j) for j in (0, 1, 2)}
    early = jnp.where(col == jnp.where(sub < 2, 2, 1), leg, rest)

    turn = [
        (at(s, r, c), at(r // 4, 4 * s + c, r % 4)) for s in range(4) for r in range(16) for c in range(4)
    ]
    turned = lax.ppermute(mine, MESH, turn)
    turned, sent = lax.optimization_barrier((turned, sent))

    def spread(turned):
        return lax.all_to_all(jnp.broadcast_to(turned, (16,) + turned.shape), "row", 0, 0)

    right = lax.cond(
        child_map[0, 0] >= 0, spread, lambda turned: jnp.zeros((16,) + turned.shape, F32), turned
    )
    left = lax.all_gather(mine, RING, axis=0)
    partial = update(ids, child_map, front_in, early, left, right)
    return finish(ids, child_map, partial, [arrived[j] if j in arrived else send(j) for j in range(4)] + [relayed])


def solution(mesh):
    in_specs = (P("row", ("sub", "col")), P("sub", "row", "col"), P("sub", "row", "col"), P(), P())
    out_specs = P("row", ("sub", "col"))
    return jax.shard_map(shards, mesh=mesh, in_specs=in_specs, out_specs=out_specs, check_vma=False)
```

```python
import jax
import jax.numpy as jnp
from jax import lax
from jax.experimental import pallas as pl
from jax.experimental.pallas import tpu as pltpu
from jax.sharding import PartitionSpec as P

BLK = 256
PANEL = 1024
RING = ("sub", "col")
MESH = ("sub", "row", "col")
SMEM = pl.BlockSpec(memory_space=pltpu.SMEM)
VMEM = pl.BlockSpec(memory_space=pltpu.VMEM)
PARAMS = pltpu.CompilerParams(vmem_limit_bytes=56 * 1024 * 1024)
F32 = jnp.float32


def split(x):
    hi = x.astype(jnp.bfloat16)
    return hi, (x - hi.astype(F32)).astype(jnp.bfloat16)


def place(cmap, child, group, slot):
    target = 3 * group + slot
    first = (cmap[child, 2 * group] == target).astype(jnp.int32)
    second = (cmap[child, 2 * group + 1] == target).astype(jnp.int32)
    return second, first + second


def mask_kernel(ids, pat, *refs):
    i = pl.program_id(0)
    for j in range(4):
        group = (ids[0] + j) % 4
        for b in range(2):
            cols = pl.ds(b * BLK, BLK)
            refs[4 + j][:, cols] = refs[j][0, :, cols] * pat[i, 2 * group + b].astype(F32)


def masked_groups(ids, pat, child):
    def group(j):
        return pl.BlockSpec((1, BLK, 2 * BLK), lambda i, ids, pat: (0, i, (ids[0] + j) % 4))

    return pl.pallas_call(
        mask_kernel,
        grid_spec=pltpu.PrefetchScalarGridSpec(
            num_scalar_prefetch=2,
            grid=(2,),
            in_specs=[group(j) for j in range(4)],
            out_specs=[pl.BlockSpec((BLK, 2 * BLK), lambda i, ids, pat: (i, 0))] * 4,
        ),
        out_shape=[jax.ShapeDtypeStruct((2 * BLK, 2 * BLK), F32)] * 4,
        compiler_params=PARAMS,
        name="masked_groups",
    )(ids, pat, child, child, child, child)


def panel_kernel(ids, pat, cmap, child, front, last, *outs):
    s = ids[0]
    row = ids[1]
    root = (s == 0).astype(F32)
    cols = [place(cmap, s, 0, q) for q in range(3)]
    cols.append((jnp.int32(2), (cmap[s, 2] == 3).astype(jnp.int32)))
    for p in range(3):
        a, a_ok = place(cmap, s, row, p)
        for q in range(4):
            b, b_ok = cols[q]
            weight = (pat[a, b] * a_ok * b_ok).astype(F32)
            for d in range(4):
                t = (s + d) % 4
                src = pl.multiple_of(a * BLK + t * 64, 64)
                own = pl.ds(pl.multiple_of(p * BLK + t * 64, 64), 64)
                value = child[0, pl.ds(src, 64), pl.ds(pl.multiple_of(b * BLK, BLK), BLK)] * weight
                kept = front[own, pl.ds(q * BLK, BLK)] if q < 3 else last[own, :]
                outs[d][p, :, pl.ds(q * BLK, BLK)] = value + kept * root


def panel_slices(ids, pat, cmap, child, front, last):
    return pl.pallas_call(
        panel_kernel,
        grid=(1,),
        in_specs=[
            SMEM,
            SMEM,
            SMEM,
            pl.BlockSpec((1, 2 * BLK, 3 * BLK), lambda i: (0, 0, 0)),
            pl.BlockSpec((3 * BLK, 3 * BLK), lambda i: (0, 0)),
            pl.BlockSpec((3 * BLK, BLK), lambda i: (0, 0)),
        ],
        out_specs=[pl.BlockSpec((3, 64, PANEL), lambda i: (0, 0, 0))] * 4,
        out_shape=[jax.ShapeDtypeStruct((3, 64, PANEL), F32)] * 4,
        compiler_params=PARAMS,
        name="panel_slices",
    )(ids, pat, cmap, child, front, last)


def pivot_kernel(pivot, hi, lo):
    hi[...], lo[...] = split(pivot[...].T)


def split_pivot(pivot):
    return pl.pallas_call(
        pivot_kernel,
        in_specs=[VMEM],
        out_specs=[VMEM, VMEM],
        out_shape=[jax.ShapeDtypeStruct((PANEL, PANEL), jnp.bfloat16)] * 2,
        compiler_params=PARAMS,
        name="split_pivot",
    )(pivot)


def dot(a, b):
    return lax.dot_general(a, b, (((1,), (1,)), ((), ())), preferred_element_type=F32)


def times(a, b):
    return lax.dot_general(a, b, (((1,), (0,)), ((), ())), preferred_element_type=F32)


def factor_kernel(*refs):
    parts, pivot_hi, pivot_lo, outs = refs[:4], refs[4], refs[5], refs[6:]
    value = parts[0][...]
    for ref in parts[1:]:
        value = value + ref[...]
    hi, lo = split(value.reshape(192, PANEL))
    ph, po = pivot_hi[...], pivot_lo[...]
    factor = (times(hi, po) + times(lo, ph) + times(hi, ph)).reshape(3, 64, PANEL)
    for k in range(4):
        outs[k][...] = factor[:, 16 * k : 16 * k + 16]


def factor_slices(parts, pivot):
    return pl.pallas_call(
        factor_kernel,
        in_specs=[VMEM] * 6,
        out_specs=[VMEM] * 4,
        out_shape=[jax.ShapeDtypeStruct((3, 16, PANEL), F32)] * 4,
        compiler_params=PARAMS,
        name="factor_slices",
    )(*parts, *pivot)


def region(ids, p, q):
    row_block = 3 * ids[1] + p
    col_block = 3 * (4 * ids[0] + ids[2]) + q
    return row_block >= 4, col_block


def sender(ids, j):
    if j == 5:
        return jnp.where(ids[0] == 1, 2, jnp.where(ids[0] == 2, 1, ids[0]))
    return (ids[2] - j + 4) % 4


def lands(ids, cmap, j, p, q):
    child = sender(ids, j)
    group = 4 * ids[0] + ids[2]
    return (place(cmap, child, ids[1], p)[1] * place(cmap, child, group, q)[1]).astype(F32)


def update_kernel(ids, cmap, front, early, *refs):
    left, right, out = refs[:3]
    left_hi, left_lo, right_hi, right_lo = refs[3:]
    p = pl.program_id(0)
    q = pl.program_id(1)

    @pl.when(q == 0)
    def _():
        hi, lo = split(left[...].reshape(BLK, PANEL))
        left_hi[...] = hi
        left_lo[...] = lo

    @pl.when(p == 0)
    def _():
        hi, lo = split(right[...].reshape(BLK, PANEL))
        right_hi[q] = hi
        right_lo[q] = lo

    value = front[...] + early[...] * lands(ids, cmap, 5, p, q)
    below, col_block = region(ids, p, q)
    out[...] = value

    @pl.when(below & (col_block < 4))
    def _():
        cols = pl.ds(pl.multiple_of(jnp.minimum(col_block, 3) * BLK, BLK), BLK)
        out[...] = left[:, 0, :, cols].reshape(BLK, BLK)

    @pl.when(below & (col_block >= 4))
    def _():
        lh, ll, rh, rl = left_hi[...], left_lo[...], right_hi[q], right_lo[q]
        out[...] = value - (dot(lh, rl) + dot(ll, rh) + dot(lh, rh))


def update(ids, cmap, front, early, left, right):
    def where(p, q, ids, cmap):
        child = sender(ids, 5)
        return (
            place(cmap, child, ids[1], p)[0],
            place(cmap, child, 4 * ids[0] + ids[2], q)[0],
        )

    tile = pl.BlockSpec((BLK, BLK), lambda p, q, ids, cmap: (p, q))
    return pl.pallas_call(
        update_kernel,
        grid_spec=pltpu.PrefetchScalarGridSpec(
            num_scalar_prefetch=2,
            grid=(3, 3),
            in_specs=[tile, pl.BlockSpec((BLK, BLK), where)]
            + [pl.BlockSpec((16, 1, 16, PANEL), lambda p, q, ids, cmap: (0, p, 0, 0))]
            + [
                pl.BlockSpec(
                    (16, 1, 16, PANEL), lambda p, q, ids, cmap: (0, jnp.where(p == 0, q, 2), 0, 0)
                )
            ],
            out_specs=tile,
            scratch_shapes=[
                pltpu.VMEM((BLK, PANEL), jnp.bfloat16),
                pltpu.VMEM((BLK, PANEL), jnp.bfloat16),
                pltpu.VMEM((3, BLK, PANEL), jnp.bfloat16),
                pltpu.VMEM((3, BLK, PANEL), jnp.bfloat16),
            ],
        ),
        out_shape=jax.ShapeDtypeStruct((3 * BLK, 3 * BLK), F32),
        compiler_params=PARAMS,
        name="update",
    )(ids, cmap, front, early, left, right)


def finish_kernel(ids, cmap, partial, r0, r1, r2, r3, r4, out):
    p = pl.program_id(0) // 2
    group = 4 * ids[0] + ids[2]
    for q in range(3):
        cols = pl.ds(q * BLK, BLK)
        below, col_block = region(ids, p, q)
        kept = jnp.where(below & (col_block < 4), 0.0, 1.0)
        value = partial[:, cols]
        for j, ref in ((0, r0), (1, r1), (2, r2), (3, r3), (2, r4)):
            b = place(cmap, sender(ids, j), group, q)[0]
            src = pl.ds(pl.multiple_of(b * BLK, BLK), BLK)
            value = value + ref[:, src] * (lands(ids, cmap, j, p, q) * kept)
        out[:, cols] = value


def finish(ids, cmap, partial, arrived):
    def arrival(j):
        return pl.BlockSpec(
            (BLK // 2, 2 * BLK),
            lambda i, ids, cmap: (2 * place(cmap, sender(ids, j), ids[1], i // 2)[0] + i % 2, 0),
        )

    band = pl.BlockSpec((BLK // 2, 3 * BLK), lambda i, ids, cmap: (i, 0))
    return pl.pallas_call(
        finish_kernel,
        grid_spec=pltpu.PrefetchScalarGridSpec(
            num_scalar_prefetch=2,
            grid=(6,),
            in_specs=[band] + [arrival(j) for j in (0, 1, 2, 3, 2)],
            out_specs=band,
        ),
        out_shape=jax.ShapeDtypeStruct((3 * BLK, 3 * BLK), F32),
        compiler_params=PARAMS,
        name="finish",
    )(ids, cmap, partial, *arrived)


def shards(front_in, child_updates, pattern, child_map, pivot_inverse):
    sub = lax.axis_index("sub")
    row = lax.axis_index("row")
    col = lax.axis_index("col")
    ids = jnp.stack([sub, row, col]).astype(jnp.int32)
    pat = pattern[0]

    def at(s, r, c):
        return (s * 16 + r) * 4 + c

    ahead = [
        [(0, 0, 2, (0, 2)), (3, 3, 1, (3, 1)), (1, 2, 1, (2, 1)), (2, 1, 2, (1, 2)), (3, 1, 1, (2, 2)), (0, 2, 2, (1, 1))],
        [(0, 0, 3, (0, 3)), (3, 3, 0, (3, 0)), (1, 2, 0, (2, 0)), (2, 1, 3, (1, 3))],
    ]
    gone = {(s, c, k) for part in ahead for s, c, k, _ in part}

    def send(j):
        pairs = []
        for s in range(4):
            for r in range(16):
                for c in range(4):
                    k = (s + j) % 4
                    if (r < 2 or c + k > 0) and (s, c, k) not in gone:
                        pairs.append((at(s, r, c), at(c, r, k)))
        return lax.ppermute(sent[j], MESH, pairs)

    def send_ahead(block, part):
        return lax.ppermute(
            block, MESH, [(at(s, r, c), at(t[0], r, t[1])) for s, c, _, t in part for r in range(16)]
        )

    last = lax.ppermute(front_in[:, :BLK], RING, [(1, 0)])
    sent = masked_groups(ids, pat, child_updates)
    slices = panel_slices(ids, pat, child_map, child_updates, front_in, last)
    parts = [slices[0]]
    for d in range(1, 4):
        parts.append(lax.ppermute(slices[d], RING, [(4 * s, 4 * ((s + d) % 4)) for s in range(4)]))
    pieces = factor_slices(parts, split_pivot(pivot_inverse))
    mine = pieces[0]
    others = [lax.ppermute(pieces[k], RING, [(4 * s, 4 * s + k) for s in range(4)]) for k in range(1, 4)]
    mine = jnp.where(col == 0, mine, others[0] + others[1] + others[2])

    leg = send_ahead(jnp.where((sub == 0) | (sub == 3), sent[2], sent[0]), ahead[0])
    rest = send_ahead(jnp.where(sub < 2, sent[3], sent[1]), ahead[1])
    mine, leg, rest, sent = lax.optimization_barrier((mine, leg, rest, sent))
    relayed = lax.ppermute(
        leg, MESH, [(at(s, r, s), at(3 - s, r, 3 - s)) for s in (1, 2) for r in range(16)]
    )
    arrived = {j: send(j) for j in (0, 1, 2)}
    early = jnp.where(col == jnp.where(sub < 2, 2, 1), leg, rest)

    turn = [
        (at(s, r, c), at(r // 4, 4 * s + c, r % 4)) for s in range(4) for r in range(16) for c in range(4)
    ]
    turned = lax.ppermute(mine, MESH, turn)
    turned, sent = lax.optimization_barrier((turned, sent))

    def spread(turned):
        return lax.all_to_all(jnp.broadcast_to(turned, (16,) + turned.shape), "row", 0, 0)

    right = lax.cond(
        child_map[0, 0] >= 0, spread, lambda turned: jnp.zeros((16,) + turned.shape, F32), turned
    )
    left = lax.all_gather(mine, RING, axis=0)
    partial = update(ids, child_map, front_in, early, left, right)
    return finish(ids, child_map, partial, [arrived[j] if j in arrived else send(j) for j in range(4)] + [relayed])


def solution(mesh):
    in_specs = (P("row", ("sub", "col")), P("sub", "row", "col"), P("sub", "row", "col"), P(), P())
    out_specs = P("row", ("sub", "col"))
    return jax.shard_map(shards, mesh=mesh, in_specs=in_specs, out_specs=out_specs, check_vma=False)
```
